32 devices in a mesh: grp: 2 (over x), tile: 8 (over z, y), freq: 2 (over core).
Axes of the slice: x: 2, y: 2, z: 4, core: 2. Of those that a mesh axis runs over, the one named last changes fastest.
Arguments:
- green_recv: bfloat16 [4, 2, 1024, 4096], P(('grp', 'freq'), None, None, 'tile'), parts along dimension 0, may hold values from -2 to 2
- green_shot: bfloat16 [4, 2, 512, 4096], P(('grp', 'freq'), None, None, 'tile'), parts along dimension 0, may hold values from -2.5 to 2.5
- band_mask: int32 [16, 5], P('grp'), parts along dimension 0, may hold values from 0 to 1, as said below
- live_counts: int32 [16], P('grp'), parts along dimension 0, may hold values from 128 to 512, as said below
- freq_bins: int32 [4], P(('grp', 'freq')), parts along dimension 0, may hold values from 256 to 511
Outputs:
- hessian: float32 [8192, 5, 512], P(('grp', 'tile', 'freq')), parts along dimension 0
The draws below stay inside these ranges and needn't reach their ends.
There are 2 independent parts, one for each index of `grp`. The reference program is written for one: setup_inputs(seed, part) draws one part's arguments, and reference() takes and returns one part's arrays. A program takes and returns all parts, laid end to end along the dimension named above; each array names one. Nothing has to cross between parts.
Inputs may be any that keep to these rules, and one draw needn't show every extreme that they name: band_mask[t, 2 + d] equals band_mask[t + d, 2 - d], is 1 at d = 0, is 0 where t + d lies outside the tiles, and some tile has all 5 slots at 1. `live_counts`: some tile has all 512 points live.
All inputs are finite; a program needn't handle non-finite values.
Results may differ from the reference program's by a relative error of at most 0.00065.
Values may be sent and summed in bfloat16 or wider, within the bound.
A program may use at most 64 MiB of HBM per device.

```python
import jax
import jax.numpy as jnp
from jax import lax

RECV = 1024
SHOTS = 512
PTS = 512
REACH = 2
BINS = 512
TILES = 8
FREQS = 2
BAND = 5


def draw_band_mask(key, part):
    first_key, second_key = jax.random.split(jax.random.fold_in(key, 11))
    upper = jax.random.randint(first_key, (TILES, REACH), 0, 2, dtype=jnp.int32)
    center = jax.random.randint(second_key, (), REACH, TILES - REACH, dtype=jnp.int32)
    rows = jnp.arange(TILES, dtype=jnp.int32)[:, None]
    spans = jnp.arange(1, REACH + 1, dtype=jnp.int32)[None, :]
    upper = jnp.where((rows == center) | (rows + spans == center), 1, upper)
    upper = jnp.where(rows + spans < TILES, upper, 0)
    lower_cols = []
    upper_cols = []
    for distance in range(1, REACH + 1):
        column = upper[:, distance - 1]
        upper_cols.append(column)
        lower_cols.append(jnp.concatenate([jnp.zeros((distance,), jnp.int32), column[:TILES - distance]]))
    columns = lower_cols[::-1] + [jnp.ones((TILES,), jnp.int32)] + upper_cols
    return jnp.stack(columns, axis=1).astype(jnp.int32)


def draw_live_counts(key, part):
    first_key, second_key = jax.random.split(jax.random.fold_in(key, 23))
    counts = jax.random.randint(first_key, (TILES,), PTS // 4, PTS + 1, dtype=jnp.int32)
    full_tile = jax.random.randint(second_key, (), 0, TILES, dtype=jnp.int32)
    return jnp.where(jnp.arange(TILES, dtype=jnp.int32) == full_tile, PTS, counts).astype(jnp.int32)


def block_scale(stream_key, extent, cuts, smallest, largest):
    loudness = 1.0
    for position, blocks in cuts:
        heights = jax.random.uniform(jax.random.fold_in(jax.random.fold_in(stream_key, 6), position), (blocks,), jnp.float32, smallest / len(cuts), largest / len(cuts))
        loudness = loudness * jnp.repeat(jnp.exp(heights), extent[position] // blocks).reshape((-1,) + (1,) * (len(extent) - 1 - position))
    return loudness


def centred(stream_key, extent, deviation, reach, cuts=(), kind=jnp.bfloat16):
    drawn = deviation * jax.random.normal(stream_key, extent, jnp.float32)
    if cuts:
        drawn = drawn * block_scale(stream_key, extent, cuts, -0.22, 0.18)
    return jnp.clip(drawn, -reach, reach).astype(kind)


def setup_inputs(seed: int = 0, part: int = 0) -> dict:
    keys = jax.random.split(jax.random.key(seed), 6)
    part_splits = jax.random.split(jax.random.fold_in(keys[5], part), 6)
    green_recv = centred(part_splits[0], (FREQS, 2, RECV, TILES * PTS), 0.15, 2.0, ((0, 2), (3, 8)))
    green_shot = centred(part_splits[1], (FREQS, 2, SHOTS, TILES * PTS), 0.177, 2.5, ((0, 2), (3, 8)))
    band_mask = draw_band_mask(jax.random.fold_in(jax.random.fold_in(keys[5], part), 71), part)
    live_counts = draw_live_counts(jax.random.fold_in(jax.random.fold_in(keys[5], part), 71), part)
    freq_bins = jax.random.randint(part_splits[4], (FREQS,), BINS // 2, BINS).astype(jnp.int32)
    return {"green_recv": green_recv, "green_shot": green_shot, "band_mask": band_mask, "live_counts": live_counts, "freq_bins": freq_bins}


def shift_tiles(field, distance):
    if distance == 0:
        return field
    count = field.shape[-2]
    if distance > 0:
        moved = field[..., distance:, :]
        empty = jnp.zeros(field.shape[:-2] + (distance, field.shape[-1]), field.dtype)
        return jnp.concatenate([moved, empty], axis=-2)
    moved = field[..., :count + distance, :]
    empty = jnp.zeros(field.shape[:-2] + (-distance, field.shape[-1]), field.dtype)
    return jnp.concatenate([empty, moved], axis=-2)


def gram_pair(left_block, right_block):
    product = jnp.einsum("fcrti,fdrtj->tfcidj", left_block, right_block, precision=lax.Precision.HIGHEST)
    real_part = product[:, :, 0, :, 0] + product[:, :, 1, :, 1]
    imag_part = product[:, :, 1, :, 0] - product[:, :, 0, :, 1]
    return real_part, imag_part


def reference(green_recv, green_shot, band_mask, live_counts, freq_bins):
    recv_all = green_recv.astype(jnp.float32).reshape(FREQS, 2, RECV, TILES, PTS)
    shot_all = green_shot.astype(jnp.float32).reshape(FREQS, 2, SHOTS, TILES, PTS)
    weights = (freq_bins.astype(jnp.float32) / BINS) ** 4
    live_mask = (jnp.arange(PTS, dtype=jnp.int32)[None, :] < live_counts[:, None]).astype(jnp.float32)
    blocks = []
    for offset in range(-REACH, REACH + 1):
        recv_real, recv_imag = gram_pair(recv_all, shift_tiles(recv_all, offset))
        shot_real, shot_imag = gram_pair(shot_all, shift_tiles(shot_all, offset))
        summed = jnp.einsum("f,tfij->tij", weights, recv_real * shot_real - recv_imag * shot_imag,
                            precision=lax.Precision.HIGHEST)
        far_live = shift_tiles(live_mask, offset)
        active = band_mask[:, REACH + offset].astype(jnp.float32)
        blocks.append(summed * active[:, None, None] * live_mask[:, :, None] * far_live[:, None, :])
    hessian = jnp.stack(blocks, axis=2)
    return hessian.reshape(TILES * PTS, BAND, PTS)
```

```python
import functools

import jax
import jax.numpy as jnp
from jax import lax
from jax.experimental import pallas as pl
from jax.experimental.pallas import tpu as pltpu
from jax.sharding import PartitionSpec as P

BINS = 512
VMEM_MIB = 44
MESH = pl.DeviceIdType.MESH
PAIR = {(1, 0): 0, (2, 0): 1, (2, 1): 2, (1, 2): 2}
ROW = {1: 0, 2: 1, -1: 2, -2: 3}


def place(tiles):
    t = lax.axis_index("tile")
    f = lax.axis_index("freq")
    step = 1 - 2 * f
    r = f * (tiles - 1) + step * t
    return t, f, step, r, lax.rem(r, 2) == 0


def band_kernel(tiles, radius, recv_ref, shot_ref, bins_ref, band_hbm, live_hbm, out,
                band_ref, live_ref, table_sem, inbox, far_r, far_s, left_r, left_s, own, self_out, self_in, outbox, turned,
                own_sem, data_send, data_recv, res_send, res_recv, self_send, self_recv):
    t, f, step, r, heavy = place(tiles)
    depth_r, points = recv_ref.shape
    depth_s = shot_ref.shape[0]
    half = points // 2
    part = half // 2
    has_far = r + 2 < tiles
    tables = [pltpu.make_async_copy(src, dst, table_sem.at[k]) for k, (src, dst) in enumerate(
        ((band_hbm, band_ref), (live_hbm, live_ref)))]
    for table in tables:
        table.start()

    def columns(j):
        return pl.ds(pl.multiple_of(j * half, half), half)

    def parts(i):
        return pl.ds(pl.multiple_of(i * part, part), part)

    def own_copy(which, j):
        src, dst = ((recv_ref, far_r), (shot_ref, far_s))[which]
        return pltpu.make_async_copy(src.at[:, columns(j)], dst.at[0, j], own_sem.at[which, j])

    def data_copy(which, i, distance):
        src, dst = ((recv_ref, far_r), (shot_ref, far_s))[which]
        return pltpu.make_async_remote_copy(
            src_ref=src.at[:, parts(i)], dst_ref=dst.at[distance, i // 2, :, parts(i % 2)],
            send_sem=data_send.at[which, i, distance - 1], recv_sem=data_recv.at[which, i, distance - 1],
            device_id={"tile": t - step * distance}, device_id_type=MESH)

    barrier = pltpu.get_barrier_semaphore()
    for distance in range(-2, 3):
        near = t + distance
        for turn in range(2):
            if distance == 0 and turn == 0:
                continue
            other = f if turn == 0 else 1 - f

            @pl.when((near >= 0) & (near < tiles))
            def _():
                pl.semaphore_signal(barrier, inc=1, device_id={"tile": near, "freq": other}, device_id_type=MESH)
    reached = jnp.minimum(t, 2) + jnp.minimum(tiles - 1 - t, 2)
    for j in range(2):
        for which in range(2):
            own_copy(which, j).start()

    pl.semaphore_wait(barrier, 2 * reached + 1)

    for i in range(4):
        for which in range(2):
            @pl.when(jnp.logical_not(heavy))
            def _():
                data_copy(which, i, 1).start()

            @pl.when(r >= 2)
            def _():
                data_copy(which, i, 2).start()

    def build_left(slot, i):
        for src, dst, depth in ((far_r, left_r, depth_r // 2), (far_s, left_s, depth_s // 2)):
            re = src[slot, i // 2, 0:depth, parts(i % 2)].T
            im = src[slot, i // 2, depth:2 * depth, parts(i % 2)].T
            dst[slot, i, 0:part, 0:depth] = re
            dst[slot, i, 0:part, depth:2 * depth] = im
            dst[slot, i, part:half, 0:depth] = im
            dst[slot, i, part:half, depth:2 * depth] = -re

    def block(left, i, right, h):
        rr = jnp.dot(left_r[left, i], far_r[right, h], preferred_element_type=jnp.float32)
        ss = jnp.dot(left_s[left, i], far_s[right, h], preferred_element_type=jnp.float32)
        return (rr[:part] * ss[:part] - rr[part:] * ss[part:]) * weight

    def origin_at(h):
        return jnp.where(h == f, 0, 1)

    def plain_send(left, i, right, h, n):
        k, origin, row = PAIR[left, right], origin_at(i // 2), ROW[right - left]
        return pltpu.make_async_remote_copy(
            src_ref=outbox.at[k, n], dst_ref=inbox.at[origin, row, parts(i % 2), columns(h)],
            send_sem=res_send.at[k, 0], recv_sem=res_recv.at[origin, row],
            device_id={"tile": t + step * left, "freq": i // 2}, device_id_type=MESH)

    def turned_send(left, i, right, h, n):
        k, origin, row = PAIR[left, right], origin_at(h), ROW[left - right]
        return pltpu.make_async_remote_copy(
            src_ref=turned.at[k, n], dst_ref=inbox.at[origin, row, :, parts(i)],
            send_sem=res_send.at[k, 1], recv_sem=res_recv.at[origin, row],
            device_id={"tile": t + step * right, "freq": h}, device_id_type=MESH)

    def unit(left, i, right, h, n, send):
        k = PAIR[left, right]
        value = block(left, i, right, h)
        outbox[k, n] = value.astype(jnp.bfloat16)
        if send:
            plain_send(left, i, right, h, n).start()
        if right == 0:
            @pl.when(h == f)
            def _():
                own[left, :, parts(i)] = value.T

            @pl.when(h != f)
            def _():
                turned[k, n] = value.T.astype(jnp.bfloat16)
                turned_send(left, i, right, h, n).start()
        else:
            turned[k, n] = value.T.astype(jnp.bfloat16)
            if send:
                turned_send(left, i, right, h, n).start()

    def self_copy():
        return pltpu.make_async_remote_copy(
            src_ref=self_out, dst_ref=self_in, send_sem=self_send, recv_sem=self_recv,
            device_id={"freq": 1 - f}, device_id_type=MESH)

    for j in range(2):
        for which in range(2):
            own_copy(which, j).wait()

    @pl.loop(0, 4)
    def _(i):
        build_left(0, i)

    for table in tables:
        table.wait()
    weight_root = bins_ref[0].astype(jnp.float32) / BINS
    weight = (weight_root * weight_root) * (weight_root * weight_root)

    for target, dest in ((1 - f, self_out), (f, own.at[0])):
        @pl.loop(0, 4)
        def _(m):
            dest[parts(m // 2), columns(m % 2)] = block(0, 2 * target + m // 2, 0, m % 2)

        if dest is self_out:
            self_copy().start()

    def mixed(first, bound, send):
        @pl.loop(first, bound)
        def _(n):
            unit(2, n // 2, 1, n % 2, n, send)

    @pl.loop(0, 3)
    def _(i):
        @pl.when(heavy)
        def _():
            for which in range(2):
                data_copy(which, i, 1).wait_recv()
            build_left(1, i)

            @pl.loop(0, 2)
            def _(h):
                unit(1, i, 0, h, 2 * i + h, False)

        @pl.when(heavy & has_far & (i == 2))
        def _():
            unit(1, i, 2, 0, 1, False)

        @pl.when(has_far)
        def _():
            for which in range(2):
                data_copy(which, i, 2).wait_recv()
            build_left(2, i)

            @pl.loop(0, 2)
            def _(h):
                unit(2, i, 0, h, 2 * i + h, False)

        @pl.when(heavy & has_far)
        def _():
            @pl.loop(0, jnp.where(i == 1, 2, jnp.where(i == 0, 0, 1)))
            def _(m):
                n = jnp.where(i == 1, 2 * m, 4)
                unit(2, n // 2, 1, n % 2, n, False)

    @pl.when(heavy)
    def _():
        for which in range(2):
            data_copy(which, 3, 1).wait_recv()

        @pl.loop(0, 6)
        def _(n):
            plain_send(1, n // 2, 0, n % 2, n).start()

        @pl.when(has_far)
        def _():
            plain_send(1, 2, 2, 0, 1).start()

            @pl.loop(0, 3)
            def _(m):
                turned_send(2, m, 1, 0, 2 * m).start()

        build_left(1, 3)

        @pl.loop(0, 2)
        def _(h):
            unit(1, 3, 0, h, 6 + h, True)

    @pl.when(has_far)
    def _():
        for which in range(2):
            data_copy(which, 3, 2).wait_recv()

        @pl.loop(0, 6)
        def _(n):
            plain_send(2, n // 2, 0, n % 2, n).start()

        @pl.when(heavy)
        def _():
            turned_send(1, 2, 2, 0, 1).start()

            @pl.loop(0, 3)
            def _(m):
                plain_send(2, m, 1, 0, 2 * m).start()

            unit(1, 3, 2, 0, 3, True)

        build_left(2, 3)

        @pl.loop(0, 2)
        def _(h):
            unit(2, 3, 0, h, 6 + h, True)

        @pl.when(heavy)
        def _():
            @pl.loop(5, 8)
            def _(n):
                unit(2, n // 2, 1, n % 2, n, True)

    rows = lax.broadcasted_iota(jnp.int32, (half, points), 0) + f * half
    cols = lax.broadcasted_iota(jnp.int32, (half, points), 1)
    row_live = rows < live_ref[t]

    def wait_inbox(origin, row):
        pltpu.make_async_remote_copy(
            src_ref=inbox.at[origin, row], dst_ref=inbox.at[origin, row],
            send_sem=res_send.at[0, 0], recv_sem=res_recv.at[origin, row],
            device_id={"freq": 1 - f}, device_id_type=MESH).wait_recv()

    def emit(delta, value):
        near, slot = t + step * delta, radius + step * delta
        keep = row_live & (cols < live_ref[near]) & (band_ref[t, slot] > 0)
        out[slot] = jnp.where(keep, value, 0.0)

    self_copy().wait_recv()
    emit(0, own[0] + self_in[...])
    for delta in ROW:
        exists = (r + delta >= 0) & (r + delta < tiles)

        @pl.when(jnp.logical_not(exists))
        def _():
            out[radius + step * delta] = jnp.zeros((half, points), jnp.float32)

    for delta in (2, -2, 1, -1):
        row = ROW[delta]
        exists = (r + delta >= 0) & (r + delta < tiles)

        def own_sum():
            wait_inbox(1, ROW[-delta])
            emit(delta, own[delta] + inbox[1, ROW[-delta]].astype(jnp.float32))

        def inbox_sum():
            wait_inbox(0, row)
            wait_inbox(1, ROW[-delta])
            emit(delta, inbox[0, row].astype(jnp.float32) + inbox[1, ROW[-delta]].astype(jnp.float32))

        if delta == 2:
            pl.when(exists)(own_sum)
        elif delta == 1:
            pl.when(exists & heavy)(own_sum)
            pl.when(exists & jnp.logical_not(heavy))(inbox_sum)
        else:
            pl.when(exists)(inbox_sum)

    self_copy().wait_send()
    for i in range(4):
        for which in range(2):
            @pl.when(jnp.logical_not(heavy))
            def _():
                data_copy(which, i, 1).wait_send()

            @pl.when(r >= 2)
            def _():
                data_copy(which, i, 2).wait_send()

    def wait_sent(box, sem):
        pltpu.make_async_remote_copy(
            src_ref=box, dst_ref=box, send_sem=sem, recv_sem=res_recv.at[0, 0],
            device_id={"freq": 1 - f}, device_id_type=MESH).wait_send()

    for k, made in enumerate((heavy, has_far, heavy & has_far)):
        @pl.when(made)
        def _():
            wait_sent(outbox.at[k], res_send.at[k, 0])
            wait_sent(turned.at[k] if k == 2 else turned.at[k, 0:4], res_send.at[k, 1])


def store_kernel(band, out_ref, out_sem):
    slots = band.shape[0]
    for slot in range(slots):
        pltpu.make_async_copy(band.at[slot], out_ref.at[slot], out_sem.at[slot]).start()
    for slot in range(slots):
        pltpu.make_async_copy(band.at[slot], out_ref.at[slot], out_sem.at[slot]).wait()


def in_hbm(array):
    return pltpu.with_memory_space_constraint(array, pltpu.HBM)


def per_device(green_recv, green_shot, band_mask, live_counts, freq_bins):
    tiles = lax.axis_size("tile")
    points = green_recv.shape[3]
    slots = band_mask.shape[1]
    half = points // 2
    depth_r = 2 * green_recv.shape[2]
    depth_s = 2 * green_shot.shape[2]
    bf16, f32 = jnp.bfloat16, jnp.float32
    dma = pltpu.SemaphoreType.DMA
    anywhere = pl.BlockSpec(memory_space=pltpu.HBM)
    band = pl.pallas_call(
        functools.partial(band_kernel, tiles, slots // 2),
        out_shape=jax.ShapeDtypeStruct((slots, half, points), f32),
        in_specs=[anywhere, anywhere, pl.BlockSpec(memory_space=pltpu.SMEM), anywhere, anywhere],
        out_specs=pl.BlockSpec(memory_space=pltpu.VMEM),
        scratch_shapes=[
            pltpu.SMEM(band_mask.shape, jnp.int32),
            pltpu.SMEM(live_counts.shape, jnp.int32),
            dma((2,)),
            pltpu.VMEM((2, 4, half, points), bf16),
            pltpu.VMEM((3, 2, depth_r, half), bf16),
            pltpu.VMEM((3, 2, depth_s, half), bf16),
            pltpu.VMEM((3, 4, half, depth_r), bf16),
            pltpu.VMEM((3, 4, half, depth_s), bf16),
            pltpu.VMEM((3, half, points), f32),
            pltpu.VMEM((half, points), f32),
            pltpu.VMEM((half, points), f32),
            pltpu.VMEM((3, 8, half // 2, half), bf16),
            pltpu.VMEM((3, 8, half, half // 2), bf16),
            dma((2, 2)),
            dma((2, 4, 2)),
            dma((2, 4, 2)),
            dma((3, 2)),
            dma((2, 4)),
            dma,
            dma,
        ],
        compiler_params=pltpu.CompilerParams(
            collective_id=0, has_side_effects=True, vmem_limit_bytes=VMEM_MIB * 1024 * 1024),
    )(in_hbm(green_recv.reshape(depth_r, points)), in_hbm(green_shot.reshape(depth_s, points)), freq_bins,
      in_hbm(band_mask), in_hbm(live_counts))
    band = pl.pallas_call(
        store_kernel,
        out_shape=jax.ShapeDtypeStruct((slots, half, points), f32),
        in_specs=[pl.BlockSpec(memory_space=pltpu.VMEM)],
        out_specs=anywhere,
        scratch_shapes=[dma((slots,))],
        compiler_params=pltpu.CompilerParams(vmem_limit_bytes=4 * 1024 * 1024),
    )(band)
    return jnp.transpose(band, (1, 0, 2))


def solution(mesh):
    return jax.shard_map(
        per_device,
        mesh=mesh,
        in_specs=(
            P(("grp", "freq"), None, None, "tile"),
            P(("grp", "freq"), None, None, "tile"),
            P("grp", None),
            P("grp"),
            P(("grp", "freq")),
        ),
        out_specs=P(("grp", "tile", "freq"), None, None),
        check_vma=False,
    )
```

```python
import functools

import jax
import jax.numpy as jnp
from jax import lax
from jax.experimental import pallas as pl
from jax.experimental.pallas import tpu as pltpu
from jax.sharding import PartitionSpec as P

BINS = 512
VMEM_MIB = 44
MESH = pl.DeviceIdType.MESH
PAIR = {(1, 0): 0, (2, 0): 1, (2, 1): 2, (1, 2): 2}
ROW = {1: 0, 2: 1, -1: 2, -2: 3}


def place(tiles):
    t = lax.axis_index("tile")
    f = lax.axis_index("freq")
    step = 1 - 2 * f
    r = f * (tiles - 1) + step * t
    return t, f, step, r, lax.rem(r, 2) == 0


def band_kernel(tiles, radius, recv_ref, shot_ref, bins_ref, band_hbm, live_hbm, out,
                band_ref, live_ref, table_sem, inbox, far_r, far_s, left_r, left_s, own, self_out, self_in, outbox, turned,
                own_sem, data_send, data_recv, res_send, res_recv, self_send, self_recv):
    t, f, step, r, heavy = place(tiles)
    depth_r, points = recv_ref.shape
    depth_s = shot_ref.shape[0]
    half = points // 2
    part = half // 2
    has_far = r + 2 < tiles
    tables = [pltpu.make_async_copy(src, dst, table_sem.at[k]) for k, (src, dst) in enumerate(
        ((band_hbm, band_ref), (live_hbm, live_ref)))]
    for table in tables:
        table.start()

    def columns(j):
        return pl.ds(pl.multiple_of(j * half, half), half)

    def parts(i):
        return pl.ds(pl.multiple_of(i * part, part), part)

    def own_copy(which, j):
        src, dst = ((recv_ref, far_r), (shot_ref, far_s))[which]
        return pltpu.make_async_copy(src.at[:, columns(j)], dst.at[0, j], own_sem.at[which, j])

    def data_copy(which, i, distance):
        src, dst = ((recv_ref, far_r), (shot_ref, far_s))[which]
        return pltpu.make_async_remote_copy(
            src_ref=src.at[:, parts(i)], dst_ref=dst.at[distance, i // 2, :, parts(i % 2)],
            send_sem=data_send.at[which, i, distance - 1], recv_sem=data_recv.at[which, i, distance - 1],
            device_id={"tile": t - step * distance}, device_id_type=MESH)

    barrier = pltpu.get_barrier_semaphore()
    partner = t + step * jnp.where(heavy, 1, -1)

    def greet(tile, freq):
        pl.semaphore_signal(barrier, inc=1, device_id={"tile": tile, "freq": freq}, device_id_type=MESH)

    for near in (t - 2, t + 2):
        @pl.when((near >= 0) & (near < tiles))
        def _():
            greet(near, f)
            greet(near, 1 - f)
    greet(partner, f)
    greet(partner, 1 - f)
    greet(t, 1 - f)
    greeted = 3 + 2 * ((t >= 2).astype(jnp.int32) + (t + 2 < tiles).astype(jnp.int32))
    for j in range(2):
        for which in range(2):
            own_copy(which, j).start()

    pl.semaphore_wait(barrier, greeted)

    for i in range(4):
        for which in range(2):
            @pl.when(jnp.logical_not(heavy))
            def _():
                data_copy(which, i, 1).start()

            @pl.when(r >= 2)
            def _():
                data_copy(which, i, 2).start()

    def build_left(slot, i):
        for src, dst, depth in ((far_r, left_r, depth_r // 2), (far_s, left_s, depth_s // 2)):
            re = src[slot, i // 2, 0:depth, parts(i % 2)].T
            im = src[slot, i // 2, depth:2 * depth, parts(i % 2)].T
            dst[slot, i, 0:part, 0:depth] = re
            dst[slot, i, 0:part, depth:2 * depth] = im
            dst[slot, i, part:half, 0:depth] = im
            dst[slot, i, part:half, depth:2 * depth] = -re

    def block(left, i, right, h):
        rr = jnp.dot(left_r[left, i], far_r[right, h], preferred_element_type=jnp.float32)
        ss = jnp.dot(left_s[left, i], far_s[right, h], preferred_element_type=jnp.float32)
        return (rr[:part] * ss[:part] - rr[part:] * ss[part:]) * weight

    def origin_at(h):
        return jnp.where(h == f, 0, 1)

    def plain_send(left, i, right, h, n):
        k, origin, row = PAIR[left, right], origin_at(i // 2), ROW[right - left]
        return pltpu.make_async_remote_copy(
            src_ref=outbox.at[k, n], dst_ref=inbox.at[origin, row, parts(i % 2), columns(h)],
            send_sem=res_send.at[k, 0], recv_sem=res_recv.at[origin, row],
            device_id={"tile": t + step * left, "freq": i // 2}, device_id_type=MESH)

    def turned_send(left, i, right, h, n):
        k, origin, row = PAIR[left, right], origin_at(h), ROW[left - right]
        return pltpu.make_async_remote_copy(
            src_ref=turned.at[k, n], dst_ref=inbox.at[origin, row, :, parts(i)],
            send_sem=res_send.at[k, 1], recv_sem=res_recv.at[origin, row],
            device_id={"tile": t + step * right, "freq": h}, device_id_type=MESH)

    def unit(left, i, right, h, n, send):
        k = PAIR[left, right]
        value = block(left, i, right, h)
        outbox[k, n] = value.astype(jnp.bfloat16)
        if send:
            plain_send(left, i, right, h, n).start()
        if right == 0:
            @pl.when(h == f)
            def _():
                own[left, :, parts(i)] = value.T

            @pl.when(h != f)
            def _():
                turned[k, n] = value.T.astype(jnp.bfloat16)
                turned_send(left, i, right, h, n).start()
        else:
            turned[k, n] = value.T.astype(jnp.bfloat16)
            if send:
                turned_send(left, i, right, h, n).start()

    def self_copy():
        return pltpu.make_async_remote_copy(
            src_ref=self_out, dst_ref=self_in, send_sem=self_send, recv_sem=self_recv,
            device_id={"freq": 1 - f}, device_id_type=MESH)

    for j in range(2):
        for which in range(2):
            own_copy(which, j).wait()

    @pl.loop(0, 4)
    def _(i):
        build_left(0, i)

    for table in tables:
        table.wait()
    weight_root = bins_ref[0].astype(jnp.float32) / BINS
    weight = (weight_root * weight_root) * (weight_root * weight_root)

    for target, dest in ((1 - f, self_out), (f, own.at[0])):
        @pl.loop(0, 4)
        def _(m):
            dest[parts(m // 2), columns(m % 2)] = block(0, 2 * target + m // 2, 0, m % 2)

        if dest is self_out:
            self_copy().start()

    def mixed(first, bound, send):
        @pl.loop(first, bound)
        def _(n):
            unit(2, n // 2, 1, n % 2, n, send)

    @pl.loop(0, 3)
    def _(i):
        @pl.when(heavy)
        def _():
            for which in range(2):
                data_copy(which, i, 1).wait_recv()
            build_left(1, i)

            @pl.loop(0, 2)
            def _(h):
                unit(1, i, 0, h, 2 * i + h, False)

        @pl.when(heavy & has_far & (i == 2))
        def _():
            unit(1, i, 2, 0, 1, False)

        @pl.when(has_far)
        def _():
            for which in range(2):
                data_copy(which, i, 2).wait_recv()
            build_left(2, i)

            @pl.loop(0, 2)
            def _(h):
                unit(2, i, 0, h, 2 * i + h, False)

        @pl.when(heavy & has_far)
        def _():
            @pl.loop(0, jnp.where(i == 1, 2, jnp.where(i == 0, 0, 1)))
            def _(m):
                n = jnp.where(i == 1, 2 * m, 4)
                unit(2, n // 2, 1, n % 2, n, False)

    @pl.when(heavy)
    def _():
        data_copy(0, 3, 1).wait_recv()

        @pl.loop(0, 6)
        def _(n):
            plain_send(1, n // 2, 0, n % 2, n).start()

    @pl.when(has_far)
    def _():
        data_copy(0, 3, 2).wait_recv()

        @pl.loop(0, 6)
        def _(n):
            plain_send(2, n // 2, 0, n % 2, n).start()

    @pl.when(heavy & has_far)
    def _():
        plain_send(1, 2, 2, 0, 1).start()
        turned_send(1, 2, 2, 0, 1).start()

        @pl.loop(0, 3)
        def _(m):
            plain_send(2, m, 1, 0, 2 * m).start()
            turned_send(2, m, 1, 0, 2 * m).start()

    @pl.when(heavy)
    def _():
        data_copy(1, 3, 1).wait_recv()
        build_left(1, 3)

        @pl.loop(0, 2)
        def _(h):
            unit(1, 3, 0, h, 6 + h, True)

    @pl.when(has_far)
    def _():
        data_copy(1, 3, 2).wait_recv()

        @pl.when(heavy)
        def _():
            unit(1, 3, 2, 0, 3, True)

        build_left(2, 3)

        @pl.loop(0, 2)
        def _(h):
            unit(2, 3, 0, h, 6 + h, True)

        @pl.when(heavy)
        def _():
            @pl.loop(5, 8)
            def _(n):
                unit(2, n // 2, 1, n % 2, n, True)

    rows = lax.broadcasted_iota(jnp.int32, (half, points), 0) + f * half
    cols = lax.broadcasted_iota(jnp.int32, (half, points), 1)
    row_live = rows < live_ref[t]

    def wait_inbox(origin, row):
        pltpu.make_async_remote_copy(
            src_ref=inbox.at[origin, row], dst_ref=inbox.at[origin, row],
            send_sem=res_send.at[0, 0], recv_sem=res_recv.at[origin, row],
            device_id={"freq": 1 - f}, device_id_type=MESH).wait_recv()

    def emit(delta, value):
        near, slot = t + step * delta, radius + step * delta
        keep = row_live & (cols < live_ref[near]) & (band_ref[t, slot] > 0)
        out[slot] = jnp.where(keep, value, 0.0)

    self_copy().wait_recv()
    emit(0, own[0] + self_in[...])
    for delta in ROW:
        exists = (r + delta >= 0) & (r + delta < tiles)

        @pl.when(jnp.logical_not(exists))
        def _():
            out[radius + step * delta] = jnp.zeros((half, points), jnp.float32)

    for delta in (2, -2, 1, -1):
        row = ROW[delta]
        exists = (r + delta >= 0) & (r + delta < tiles)

        def own_sum():
            wait_inbox(1, ROW[-delta])
            emit(delta, own[delta] + inbox[1, ROW[-delta]].astype(jnp.float32))

        def inbox_sum():
            wait_inbox(0, row)
            wait_inbox(1, ROW[-delta])
            emit(delta, inbox[0, row].astype(jnp.float32) + inbox[1, ROW[-delta]].astype(jnp.float32))

        if delta == 2:
            pl.when(exists)(own_sum)
        elif delta == 1:
            pl.when(exists & heavy)(own_sum)
            pl.when(exists & jnp.logical_not(heavy))(inbox_sum)
        else:
            pl.when(exists)(inbox_sum)

    self_copy().wait_send()
    for i in range(4):
        for which in range(2):
            @pl.when(jnp.logical_not(heavy))
            def _():
                data_copy(which, i, 1).wait_send()

            @pl.when(r >= 2)
            def _():
                data_copy(which, i, 2).wait_send()

    def wait_sent(box, sem):
        pltpu.make_async_remote_copy(
            src_ref=box, dst_ref=box, send_sem=sem, recv_sem=res_recv.at[0, 0],
            device_id={"freq": 1 - f}, device_id_type=MESH).wait_send()

    for k, made in enumerate((heavy, has_far, heavy & has_far)):
        @pl.when(made)
        def _():
            wait_sent(outbox.at[k], res_send.at[k, 0])
            wait_sent(turned.at[k] if k == 2 else turned.at[k, 0:4], res_send.at[k, 1])


def store_kernel(band, out_ref, out_sem):
    slots = band.shape[0]
    for slot in range(slots):
        pltpu.make_async_copy(band.at[slot], out_ref.at[slot], out_sem.at[slot]).start()
    for slot in range(slots):
        pltpu.make_async_copy(band.at[slot], out_ref.at[slot], out_sem.at[slot]).wait()


def in_hbm(array):
    return pltpu.with_memory_space_constraint(array, pltpu.HBM)


def per_device(green_recv, green_shot, band_mask, live_counts, freq_bins):
    tiles = lax.axis_size("tile")
    points = green_recv.shape[3]
    slots = band_mask.shape[1]
    half = points // 2
    depth_r = 2 * green_recv.shape[2]
    depth_s = 2 * green_shot.shape[2]
    bf16, f32 = jnp.bfloat16, jnp.float32
    dma = pltpu.SemaphoreType.DMA
    anywhere = pl.BlockSpec(memory_space=pltpu.HBM)
    band = pl.pallas_call(
        functools.partial(band_kernel, tiles, slots // 2),
        out_shape=jax.ShapeDtypeStruct((slots, half, points), f32),
        in_specs=[anywhere, anywhere, pl.BlockSpec(memory_space=pltpu.SMEM), anywhere, anywhere],
        out_specs=pl.BlockSpec(memory_space=pltpu.VMEM),
        scratch_shapes=[
            pltpu.SMEM(band_mask.shape, jnp.int32),
            pltpu.SMEM(live_counts.shape, jnp.int32),
            dma((2,)),
            pltpu.VMEM((2, 4, half, points), bf16),
            pltpu.VMEM((3, 2, depth_r, half), bf16),
            pltpu.VMEM((3, 2, depth_s, half), bf16),
            pltpu.VMEM((3, 4, half, depth_r), bf16),
            pltpu.VMEM((3, 4, half, depth_s), bf16),
            pltpu.VMEM((3, half, points), f32),
            pltpu.VMEM((half, points), f32),
            pltpu.VMEM((half, points), f32),
            pltpu.VMEM((3, 8, half // 2, half), bf16),
            pltpu.VMEM((3, 8, half, half // 2), bf16),
            dma((2, 2)),
            dma((2, 4, 2)),
            dma((2, 4, 2)),
            dma((3, 2)),
            dma((2, 4)),
            dma,
            dma,
        ],
        compiler_params=pltpu.CompilerParams(
            collective_id=0, has_side_effects=True, vmem_limit_bytes=VMEM_MIB * 1024 * 1024),
    )(in_hbm(green_recv.reshape(depth_r, points)), in_hbm(green_shot.reshape(depth_s, points)), freq_bins,
      in_hbm(band_mask), in_hbm(live_counts))
    band = pl.pallas_call(
        store_kernel,
        out_shape=jax.ShapeDtypeStruct((slots, half, points), f32),
        in_specs=[pl.BlockSpec(memory_space=pltpu.VMEM)],
        out_specs=anywhere,
        scratch_shapes=[dma((slots,))],
        compiler_params=pltpu.CompilerParams(vmem_limit_bytes=4 * 1024 * 1024),
    )(band)
    return jnp.transpose(band, (1, 0, 2))


def solution(mesh):
    return jax.shard_map(
        per_device,
        mesh=mesh,
        in_specs=(
            P(("grp", "freq"), None, None, "tile"),
            P(("grp", "freq"), None, None, "tile"),
            P("grp", None),
            P("grp"),
            P(("grp", "freq")),
        ),
        out_specs=P(("grp", "tile", "freq"), None, None),
        check_vma=False,
    )
```

```python
import functools

import jax
import jax.numpy as jnp
from jax import lax
from jax.experimental import pallas as pl
from jax.experimental.pallas import tpu as pltpu
from jax.sharding import PartitionSpec as P

BINS = 512
VMEM_MIB = 44
MESH = pl.DeviceIdType.MESH
PAIR = {(1, 0): 0, (2, 0): 1, (2, 1): 2, (1, 2): 2}
ROW = {1: 0, 2: 1, -1: 2, -2: 3}


def place(tiles):
    t = lax.axis_index("tile")
    f = lax.axis_index("freq")
    step = 1 - 2 * f
    r = f * (tiles - 1) + step * t
    return t, f, step, r, lax.rem(r, 2) == 0


def band_kernel(tiles, radius, recv_ref, shot_ref, bins_ref, band_hbm, live_hbm, out,
                band_ref, live_ref, table_sem, inbox, far_r, far_s, left_r, left_s, own, self_out, self_in, outbox, turned,
                own_sem, data_send, data_recv, res_send, res_recv, self_send, self_recv):
    t, f, step, r, heavy = place(tiles)
    depth_r, points = recv_ref.shape
    depth_s = shot_ref.shape[0]
    half = points // 2
    part = half // 2
    has_far = r + 2 < tiles
    tables = [pltpu.make_async_copy(src, dst, table_sem.at[k]) for k, (src, dst) in enumerate(
        ((band_hbm, band_ref), (live_hbm, live_ref)))]
    for table in tables:
        table.start()

    def columns(j):
        return pl.ds(pl.multiple_of(j * half, half), half)

    def parts(i):
        return pl.ds(pl.multiple_of(i * part, part), part)

    def own_copy(which, j):
        src, dst = ((recv_ref, far_r), (shot_ref, far_s))[which]
        return pltpu.make_async_copy(src.at[:, columns(j)], dst.at[0, j], own_sem.at[which, j])

    def data_copy(which, i, distance):
        src, dst = ((recv_ref, far_r), (shot_ref, far_s))[which]
        return pltpu.make_async_remote_copy(
            src_ref=src.at[:, parts(i)], dst_ref=dst.at[distance, i // 2, :, parts(i % 2)],
            send_sem=data_send.at[which, i, distance - 1], recv_sem=data_recv.at[which, i, distance - 1],
            device_id={"tile": t - step * distance}, device_id_type=MESH)

    barrier = pltpu.get_barrier_semaphore()

    def greet(tile, freq):
        pl.semaphore_signal(barrier, inc=1, device_id={"tile": tile, "freq": freq}, device_id_type=MESH)

    pl.when(has_far)(lambda: greet(t + 2 * step, f))
    pl.when(heavy)(lambda: greet(t + step, f))
    greet(t, 1 - f)
    greeters = 1 + jnp.where(heavy, 0, 1) + jnp.where(r >= 2, 1, 0)
    for j in range(2):
        for which in range(2):
            own_copy(which, j).start()

    pl.semaphore_wait(barrier, greeters)

    for i in range(4):
        for which in range(2):
            @pl.when(jnp.logical_not(heavy))
            def _():
                data_copy(which, i, 1).start()

            @pl.when(r >= 2)
            def _():
                data_copy(which, i, 2).start()

    def build_left(slot, i):
        for src, dst, depth in ((far_r, left_r, depth_r // 2), (far_s, left_s, depth_s // 2)):
            re = src[slot, i // 2, 0:depth, parts(i % 2)].T
            im = src[slot, i // 2, depth:2 * depth, parts(i % 2)].T
            dst[slot, i, 0:part, 0:depth] = re
            dst[slot, i, 0:part, depth:2 * depth] = im
            dst[slot, i, part:half, 0:depth] = im
            dst[slot, i, part:half, depth:2 * depth] = -re

    def block(left, i, right, h):
        rr = jnp.dot(left_r[left, i], far_r[right, h], preferred_element_type=jnp.float32)
        ss = jnp.dot(left_s[left, i], far_s[right, h], preferred_element_type=jnp.float32)
        return (rr[:part] * ss[:part] - rr[part:] * ss[part:]) * weight

    def origin_at(h):
        return jnp.where(h == f, 0, 1)

    def plain_send(left, i, right, h, n):
        k, origin, row = PAIR[left, right], origin_at(i // 2), ROW[right - left]
        return pltpu.make_async_remote_copy(
            src_ref=outbox.at[k, n], dst_ref=inbox.at[origin, row, parts(i % 2), columns(h)],
            send_sem=res_send.at[k, 0], recv_sem=res_recv.at[origin, row],
            device_id={"tile": t + step * left, "freq": i // 2}, device_id_type=MESH)

    def turned_send(left, i, right, h, n):
        k, origin, row = PAIR[left, right], origin_at(h), ROW[left - right]
        return pltpu.make_async_remote_copy(
            src_ref=turned.at[k, n], dst_ref=inbox.at[origin, row, :, parts(i)],
            send_sem=res_send.at[k, 1], recv_sem=res_recv.at[origin, row],
            device_id={"tile": t + step * right, "freq": h}, device_id_type=MESH)

    def unit(left, i, right, h, n, send):
        k = PAIR[left, right]
        value = block(left, i, right, h)
        outbox[k, n] = value.astype(jnp.bfloat16)
        if send:
            plain_send(left, i, right, h, n).start()
        if right == 0:
            @pl.when(h == f)
            def _():
                own[left, :, parts(i)] = value.T

            @pl.when(h != f)
            def _():
                turned[k, n] = value.T.astype(jnp.bfloat16)
                turned_send(left, i, right, h, n).start()
        else:
            turned[k, n] = value.T.astype(jnp.bfloat16)
            if send:
                turned_send(left, i, right, h, n).start()

    def self_copy():
        return pltpu.make_async_remote_copy(
            src_ref=self_out, dst_ref=self_in, send_sem=self_send, recv_sem=self_recv,
            device_id={"freq": 1 - f}, device_id_type=MESH)

    for j in range(2):
        for which in range(2):
            own_copy(which, j).wait()

    @pl.loop(0, 4)
    def _(i):
        build_left(0, i)

    for table in tables:
        table.wait()
    weight_root = bins_ref[0].astype(jnp.float32) / BINS
    weight = (weight_root * weight_root) * (weight_root * weight_root)

    for target, dest in ((1 - f, self_out), (f, own.at[0])):
        @pl.loop(0, 4)
        def _(m):
            dest[parts(m // 2), columns(m % 2)] = block(0, 2 * target + m // 2, 0, m % 2)

        if dest is self_out:
            self_copy().start()

    def mixed(first, bound, send):
        @pl.loop(first, bound)
        def _(n):
            unit(2, n // 2, 1, n % 2, n, send)

    @pl.loop(0, 3)
    def _(i):
        @pl.when(heavy)
        def _():
            for which in range(2):
                data_copy(which, i, 1).wait_recv()
            build_left(1, i)

            @pl.loop(0, 2)
            def _(h):
                unit(1, i, 0, h, 2 * i + h, False)

        @pl.when(heavy & has_far & (i == 2))
        def _():
            unit(1, i, 2, 0, 1, False)

        @pl.when(has_far)
        def _():
            for which in range(2):
                data_copy(which, i, 2).wait_recv()
            build_left(2, i)

            @pl.loop(0, 2)
            def _(h):
                unit(2, i, 0, h, 2 * i + h, False)

        @pl.when(heavy & has_far)
        def _():
            @pl.loop(0, jnp.where(i == 1, 2, jnp.where(i == 0, 0, 1)))
            def _(m):
                n = jnp.where(i == 1, 2 * m, 4)
                unit(2, n // 2, 1, n % 2, n, False)

    @pl.when(heavy)
    def _():
        data_copy(0, 3, 1).wait_recv()

        @pl.loop(0, 6)
        def _(n):
            plain_send(1, n // 2, 0, n % 2, n).start()

    @pl.when(has_far)
    def _():
        data_copy(0, 3, 2).wait_recv()

        @pl.loop(0, 6)
        def _(n):
            plain_send(2, n // 2, 0, n % 2, n).start()

    @pl.when(heavy & has_far)
    def _():
        plain_send(1, 2, 2, 0, 1).start()
        turned_send(1, 2, 2, 0, 1).start()

        @pl.loop(0, 3)
        def _(m):
            plain_send(2, m, 1, 0, 2 * m).start()
            turned_send(2, m, 1, 0, 2 * m).start()

    @pl.when(heavy)
    def _():
        data_copy(1, 3, 1).wait_recv()
        build_left(1, 3)

        @pl.loop(0, 2)
        def _(h):
            unit(1, 3, 0, h, 6 + h, True)

    @pl.when(has_far)
    def _():
        data_copy(1, 3, 2).wait_recv()

        @pl.when(heavy)
        def _():
            unit(1, 3, 2, 0, 3, True)

        build_left(2, 3)

        @pl.loop(0, 2)
        def _(h):
            unit(2, 3, 0, h, 6 + h, True)

        @pl.when(heavy)
        def _():
            @pl.loop(5, 8)
            def _(n):
                unit(2, n // 2, 1, n % 2, n, True)

    rows = lax.broadcasted_iota(jnp.int32, (half, points), 0) + f * half
    cols = lax.broadcasted_iota(jnp.int32, (half, points), 1)
    row_live = rows < live_ref[t]

    def wait_inbox(origin, row):
        pltpu.make_async_remote_copy(
            src_ref=inbox.at[origin, row], dst_ref=inbox.at[origin, row],
            send_sem=res_send.at[0, 0], recv_sem=res_recv.at[origin, row],
            device_id={"freq": 1 - f}, device_id_type=MESH).wait_recv()

    def emit(delta, value):
        near, slot = t + step * delta, radius + step * delta
        keep = row_live & (cols < live_ref[near]) & (band_ref[t, slot] > 0)
        out[slot] = jnp.where(keep, value, 0.0)

    self_copy().wait_recv()
    emit(0, own[0] + self_in[...])
    for delta in ROW:
        exists = (r + delta >= 0) & (r + delta < tiles)

        @pl.when(jnp.logical_not(exists))
        def _():
            out[radius + step * delta] = jnp.zeros((half, points), jnp.float32)

    for delta in (2, -2, 1, -1):
        row = ROW[delta]
        exists = (r + delta >= 0) & (r + delta < tiles)

        def own_sum():
            wait_inbox(1, ROW[-delta])
            emit(delta, own[delta] + inbox[1, ROW[-delta]].astype(jnp.float32))

        def inbox_sum():
            wait_inbox(0, row)
            wait_inbox(1, ROW[-delta])
            emit(delta, inbox[0, row].astype(jnp.float32) + inbox[1, ROW[-delta]].astype(jnp.float32))

        if delta == 2:
            pl.when(exists)(own_sum)
        elif delta == 1:
            pl.when(exists & heavy)(own_sum)
            pl.when(exists & jnp.logical_not(heavy))(inbox_sum)
        else:
            pl.when(exists)(inbox_sum)

    self_copy().wait_send()
    for i in range(4):
        for which in range(2):
            @pl.when(jnp.logical_not(heavy))
            def _():
                data_copy(which, i, 1).wait_send()

            @pl.when(r >= 2)
            def _():
                data_copy(which, i, 2).wait_send()

    def wait_sent(box, sem):
        pltpu.make_async_remote_copy(
            src_ref=box, dst_ref=box, send_sem=sem, recv_sem=res_recv.at[0, 0],
            device_id={"freq": 1 - f}, device_id_type=MESH).wait_send()

    for k, made in enumerate((heavy, has_far, heavy & has_far)):
        @pl.when(made)
        def _():
            wait_sent(outbox.at[k], res_send.at[k, 0])
            wait_sent(turned.at[k] if k == 2 else turned.at[k, 0:4], res_send.at[k, 1])


def store_kernel(band, out_ref, out_sem):
    slots = band.shape[0]
    for slot in range(slots):
        pltpu.make_async_copy(band.at[slot], out_ref.at[slot], out_sem.at[slot]).start()
    for slot in range(slots):
        pltpu.make_async_copy(band.at[slot], out_ref.at[slot], out_sem.at[slot]).wait()


def in_hbm(array):
    return pltpu.with_memory_space_constraint(array, pltpu.HBM)


def per_device(green_recv, green_shot, band_mask, live_counts, freq_bins):
    tiles = lax.axis_size("tile")
    points = green_recv.shape[3]
    slots = band_mask.shape[1]
    half = points // 2
    depth_r = 2 * green_recv.shape[2]
    depth_s = 2 * green_shot.shape[2]
    bf16, f32 = jnp.bfloat16, jnp.float32
    dma = pltpu.SemaphoreType.DMA
    anywhere = pl.BlockSpec(memory_space=pltpu.HBM)
    band = pl.pallas_call(
        functools.partial(band_kernel, tiles, slots // 2),
        out_shape=jax.ShapeDtypeStruct((slots, half, points), f32),
        in_specs=[anywhere, anywhere, pl.BlockSpec(memory_space=pltpu.SMEM), anywhere, anywhere],
        out_specs=pl.BlockSpec(memory_space=pltpu.VMEM),
        scratch_shapes=[
            pltpu.SMEM(band_mask.shape, jnp.int32),
            pltpu.SMEM(live_counts.shape, jnp.int32),
            dma((2,)),
            pltpu.VMEM((2, 4, half, points), bf16),
            pltpu.VMEM((3, 2, depth_r, half), bf16),
            pltpu.VMEM((3, 2, depth_s, half), bf16),
            pltpu.VMEM((3, 4, half, depth_r), bf16),
            pltpu.VMEM((3, 4, half, depth_s), bf16),
            pltpu.VMEM((3, half, points), f32),
            pltpu.VMEM((half, points), f32),
            pltpu.VMEM((half, points), f32),
            pltpu.VMEM((3, 8, half // 2, half), bf16),
            pltpu.VMEM((3, 8, half, half // 2), bf16),
            dma((2, 2)),
            dma((2, 4, 2)),
            dma((2, 4, 2)),
            dma((3, 2)),
            dma((2, 4)),
            dma,
            dma,
        ],
        compiler_params=pltpu.CompilerParams(
            collective_id=0, has_side_effects=True, vmem_limit_bytes=VMEM_MIB * 1024 * 1024),
    )(in_hbm(green_recv.reshape(depth_r, points)), in_hbm(green_shot.reshape(depth_s, points)), freq_bins,
      in_hbm(band_mask), in_hbm(live_counts))
    band = pl.pallas_call(
        store_kernel,
        out_shape=jax.ShapeDtypeStruct((slots, half, points), f32),
        in_specs=[pl.BlockSpec(memory_space=pltpu.VMEM)],
        out_specs=anywhere,
        scratch_shapes=[dma((slots,))],
        compiler_params=pltpu.CompilerParams(vmem_limit_bytes=4 * 1024 * 1024),
    )(band)
    return jnp.transpose(band, (1, 0, 2))


def solution(mesh):
    return jax.shard_map(
        per_device,
        mesh=mesh,
        in_specs=(
            P(("grp", "freq"), None, None, "tile"),
            P(("grp", "freq"), None, None, "tile"),
            P("grp", None),
            P("grp"),
            P(("grp", "freq")),
        ),
        out_specs=P(("grp", "tile", "freq"), None, None),
        check_vma=False,
    )
```

```python
import functools

import jax
import jax.numpy as jnp
from jax import lax
from jax.experimental import pallas as pl
from jax.experimental.pallas import tpu as pltpu
from jax.sharding import PartitionSpec as P

BINS = 512
VMEM_MIB = 44
MESH = pl.DeviceIdType.MESH
PAIR = {(1, 0): 0, (2, 0): 1, (2, 1): 2, (1, 2): 2}
ROW = {1: 0, 2: 1, -1: 2, -2: 3}


def place(tiles):
    t = lax.axis_index("tile")
    f = lax.axis_index("freq")
    step = 1 - 2 * f
    r = f * (tiles - 1) + step * t
    return t, f, step, r, lax.rem(r, 2) == 0


def band_kernel(tiles, radius, recv_ref, shot_ref, bins_ref, band_hbm, live_hbm, out, inbox, own,
                band_ref, live_ref, table_sem, far_r, far_s, left_r, left_s, self_out, self_in, outbox, turned,
                own_sem, data_send, data_recv, res_send, res_recv, self_send, self_recv):
    t, f, step, r, heavy = place(tiles)
    depth_r, points = recv_ref.shape
    depth_s = shot_ref.shape[0]
    half = points // 2
    part = half // 2
    has_far = r + 2 < tiles
    tables = [pltpu.make_async_copy(src, dst, table_sem.at[k]) for k, (src, dst) in enumerate(
        ((band_hbm, band_ref), (live_hbm, live_ref)))]
    for table in tables:
        table.start()

    def columns(j):
        return pl.ds(pl.multiple_of(j * half, half), half)

    def parts(i):
        return pl.ds(pl.multiple_of(i * part, part), part)

    def own_copy(which, j):
        src, dst = ((recv_ref, far_r), (shot_ref, far_s))[which]
        return pltpu.make_async_copy(src.at[:, columns(j)], dst.at[0, j], own_sem.at[which, j])

    def data_copy(which, i, distance):
        src, dst = ((recv_ref, far_r), (shot_ref, far_s))[which]
        return pltpu.make_async_remote_copy(
            src_ref=src.at[:, parts(i)], dst_ref=dst.at[distance, i // 2, :, parts(i % 2)],
            send_sem=data_send.at[which, i, distance - 1], recv_sem=data_recv.at[which, i, distance - 1],
            device_id={"tile": t - step * distance}, device_id_type=MESH)

    barrier = pltpu.get_barrier_semaphore()

    def greet(tile, freq):
        pl.semaphore_signal(barrier, inc=1, device_id={"tile": tile, "freq": freq}, device_id_type=MESH)

    pl.when(has_far)(lambda: greet(t + 2 * step, f))
    pl.when(heavy)(lambda: greet(t + step, f))
    greet(t, 1 - f)
    greeters = 1 + jnp.where(heavy, 0, 1) + jnp.where(r >= 2, 1, 0)
    for j in range(2):
        for which in range(2):
            own_copy(which, j).start()

    pl.semaphore_wait(barrier, greeters)

    for i in range(4):
        for which in range(2):
            @pl.when(jnp.logical_not(heavy))
            def _():
                data_copy(which, i, 1).start()

            @pl.when(r >= 2)
            def _():
                data_copy(which, i, 2).start()

    def build_left(slot, i):
        for src, dst, depth in ((far_r, left_r, depth_r // 2), (far_s, left_s, depth_s // 2)):
            re = src[slot, i // 2, 0:depth, parts(i % 2)].T
            im = src[slot, i // 2, depth:2 * depth, parts(i % 2)].T
            dst[slot, i, 0:part, 0:depth] = re
            dst[slot, i, 0:part, depth:2 * depth] = im
            dst[slot, i, part:half, 0:depth] = im
            dst[slot, i, part:half, depth:2 * depth] = -re

    def block(left, i, right, h):
        rr = jnp.dot(left_r[left, i], far_r[right, h], preferred_element_type=jnp.float32)
        ss = jnp.dot(left_s[left, i], far_s[right, h], preferred_element_type=jnp.float32)
        return (rr[:part] * ss[:part] - rr[part:] * ss[part:]) * weight

    def origin_at(h):
        return jnp.where(h == f, 0, 1)

    def plain_send(left, i, right, h, n):
        k, origin, row = PAIR[left, right], origin_at(i // 2), ROW[right - left]
        return pltpu.make_async_remote_copy(
            src_ref=outbox.at[k, n], dst_ref=inbox.at[origin, row, parts(i % 2), columns(h)],
            send_sem=res_send.at[k, 0], recv_sem=res_recv.at[origin, row],
            device_id={"tile": t + step * left, "freq": i // 2}, device_id_type=MESH)

    def turned_send(left, i, right, h, n):
        k, origin, row = PAIR[left, right], origin_at(h), ROW[left - right]
        return pltpu.make_async_remote_copy(
            src_ref=turned.at[k, n], dst_ref=inbox.at[origin, row, :, parts(i)],
            send_sem=res_send.at[k, 1], recv_sem=res_recv.at[origin, row],
            device_id={"tile": t + step * right, "freq": h}, device_id_type=MESH)

    def unit(left, i, right, h, n, send):
        k = PAIR[left, right]
        value = block(left, i, right, h)
        outbox[k, n] = value.astype(jnp.bfloat16)
        if send:
            plain_send(left, i, right, h, n).start()
        if right == 0:
            @pl.when(h == f)
            def _():
                own[left, :, parts(i)] = value.T

            @pl.when(h != f)
            def _():
                turned[k, n] = value.T.astype(jnp.bfloat16)
                turned_send(left, i, right, h, n).start()
        else:
            turned[k, n] = value.T.astype(jnp.bfloat16)
            if send:
                turned_send(left, i, right, h, n).start()

    def self_copy():
        return pltpu.make_async_remote_copy(
            src_ref=self_out, dst_ref=self_in, send_sem=self_send, recv_sem=self_recv,
            device_id={"freq": 1 - f}, device_id_type=MESH)

    for j in range(2):
        for which in range(2):
            own_copy(which, j).wait()

    @pl.loop(0, 4)
    def _(i):
        build_left(0, i)

    for table in tables:
        table.wait()
    weight_root = bins_ref[0].astype(jnp.float32) / BINS
    weight = (weight_root * weight_root) * (weight_root * weight_root)

    for target, dest in ((1 - f, self_out), (f, own.at[0])):
        @pl.loop(0, 4)
        def _(m):
            dest[parts(m // 2), columns(m % 2)] = block(0, 2 * target + m // 2, 0, m % 2)

        if dest is self_out:
            self_copy().start()

    def mixed(first, bound, send):
        @pl.loop(first, bound)
        def _(n):
            unit(2, n // 2, 1, n % 2, n, send)

    @pl.loop(0, 3)
    def _(i):
        @pl.when(heavy)
        def _():
            for which in range(2):
                data_copy(which, i, 1).wait_recv()
            build_left(1, i)

            @pl.loop(0, 2)
            def _(h):
                unit(1, i, 0, h, 2 * i + h, False)

        @pl.when(heavy & has_far & (i == 2))
        def _():
            unit(1, i, 2, 0, 1, False)

        @pl.when(has_far)
        def _():
            for which in range(2):
                data_copy(which, i, 2).wait_recv()
            build_left(2, i)

            @pl.loop(0, 2)
            def _(h):
                unit(2, i, 0, h, 2 * i + h, False)

        @pl.when(heavy & has_far)
        def _():
            @pl.loop(0, jnp.where(i == 1, 2, jnp.where(i == 0, 0, 1)))
            def _(m):
                n = jnp.where(i == 1, 2 * m, 4)
                unit(2, n // 2, 1, n % 2, n, False)

    @pl.when(heavy)
    def _():
        data_copy(0, 3, 1).wait_recv()

        @pl.loop(0, 6)
        def _(n):
            plain_send(1, n // 2, 0, n % 2, n).start()

    @pl.when(has_far)
    def _():
        data_copy(0, 3, 2).wait_recv()

        @pl.loop(0, 6)
        def _(n):
            plain_send(2, n // 2, 0, n % 2, n).start()

    @pl.when(heavy & has_far)
    def _():
        plain_send(1, 2, 2, 0, 1).start()
        turned_send(1, 2, 2, 0, 1).start()

        @pl.loop(0, 3)
        def _(m):
            plain_send(2, m, 1, 0, 2 * m).start()
            turned_send(2, m, 1, 0, 2 * m).start()

    @pl.when(heavy)
    def _():
        data_copy(1, 3, 1).wait_recv()
        build_left(1, 3)

        @pl.loop(0, 2)
        def _(h):
            unit(1, 3, 0, h, 6 + h, True)

    @pl.when(has_far)
    def _():
        data_copy(1, 3, 2).wait_recv()

        @pl.when(heavy)
        def _():
            unit(1, 3, 2, 0, 3, True)

        build_left(2, 3)

        @pl.loop(0, 2)
        def _(h):
            unit(2, 3, 0, h, 6 + h, True)

        @pl.when(heavy)
        def _():
            @pl.loop(5, 8)
            def _(n):
                unit(2, n // 2, 1, n % 2, n, True)

    rows = lax.broadcasted_iota(jnp.int32, (half, points), 0) + f * half
    cols = lax.broadcasted_iota(jnp.int32, (half, points), 1)
    row_live = rows < live_ref[t]

    def wait_inbox(origin, row):
        pltpu.make_async_remote_copy(
            src_ref=inbox.at[origin, row], dst_ref=inbox.at[origin, row],
            send_sem=res_send.at[0, 0], recv_sem=res_recv.at[origin, row],
            device_id={"freq": 1 - f}, device_id_type=MESH).wait_recv()

    def kept(delta):
        near, slot = t + step * delta, radius + step * delta
        return slot, row_live & (cols < live_ref[near]) & (band_ref[t, slot] > 0)

    def emit(delta, value):
        slot, keep = kept(delta)
        out[slot] = jnp.where(keep, value, 0.0)

    for delta in (1, -1):
        @pl.when((r + delta >= 0) & (r + delta < tiles))
        def _():
            emit(delta, jnp.ones((half, points), jnp.float32))

    self_copy().wait_recv()
    emit(0, own[0] + self_in[...])
    for delta in (2, -2):
        row, mirror = ROW[delta], ROW[-delta]
        exists = (r + delta >= 0) & (r + delta < tiles)

        @pl.when(exists)
        def _():
            wait_inbox(1, mirror)
            if delta == 2:
                emit(delta, own[delta] + inbox[1, mirror].astype(jnp.float32))
            else:
                wait_inbox(0, row)
                emit(delta, inbox[0, row].astype(jnp.float32) + inbox[1, mirror].astype(jnp.float32))

        @pl.when(jnp.logical_not(exists))
        def _():
            out[radius + step * delta] = jnp.zeros((half, points), jnp.float32)

    for delta in (1, -1):
        @pl.when((r + delta >= 0) & (r + delta < tiles))
        def _():
            wait_inbox(1, ROW[-delta])
            if delta == 1:
                pl.when(jnp.logical_not(heavy))(lambda: wait_inbox(0, ROW[delta]))
            else:
                wait_inbox(0, ROW[delta])

    self_copy().wait_send()
    for i in range(4):
        for which in range(2):
            @pl.when(jnp.logical_not(heavy))
            def _():
                data_copy(which, i, 1).wait_send()

            @pl.when(r >= 2)
            def _():
                data_copy(which, i, 2).wait_send()

    def wait_sent(box, sem):
        pltpu.make_async_remote_copy(
            src_ref=box, dst_ref=box, send_sem=sem, recv_sem=res_recv.at[0, 0],
            device_id={"freq": 1 - f}, device_id_type=MESH).wait_send()

    for k, made in enumerate((heavy, has_far, heavy & has_far)):
        @pl.when(made)
        def _():
            wait_sent(outbox.at[k], res_send.at[k, 0])
            wait_sent(turned.at[k] if k == 2 else turned.at[k, 0:4], res_send.at[k, 1])


def store_kernel(tiles, band, inbox, own, out_ref, late, out_sem):
    t, f, step, r, heavy = place(tiles)
    slots, half, points = band.shape
    radius = slots // 2
    ready = [slot for slot in range(slots) if abs(slot - radius) != 1]
    copies = [pltpu.make_async_copy(band.at[slot], out_ref.at[slot], out_sem.at[slot]) for slot in ready]
    for copy in copies:
        copy.start()
    for k, delta in enumerate((1, -1)):
        slot = radius + step * delta
        exists = (r + delta >= 0) & (r + delta < tiles)

        def total(first):
            value = first + inbox[1, ROW[-delta]].astype(jnp.float32)
            late[k] = jnp.where(band[slot] > 0, value, 0.0)

        def from_inbox():
            total(inbox[0, ROW[delta]].astype(jnp.float32))

        if delta == 1:
            pl.when(exists & heavy)(lambda: total(own[1]))
            pl.when(exists & jnp.logical_not(heavy))(from_inbox)
        else:
            pl.when(exists)(from_inbox)

        @pl.when(jnp.logical_not(exists))
        def _():
            late[k] = jnp.zeros((half, points), jnp.float32)

        copies.append(pltpu.make_async_copy(late.at[k], out_ref.at[slot], out_sem.at[radius - 1 + 2 * k]))
        copies[-1].start()
    for copy in copies:
        copy.wait()


def in_hbm(array):
    return pltpu.with_memory_space_constraint(array, pltpu.HBM)


def per_device(green_recv, green_shot, band_mask, live_counts, freq_bins):
    tiles = lax.axis_size("tile")
    points = green_recv.shape[3]
    slots = band_mask.shape[1]
    half = points // 2
    depth_r = 2 * green_recv.shape[2]
    depth_s = 2 * green_shot.shape[2]
    bf16, f32 = jnp.bfloat16, jnp.float32
    dma = pltpu.SemaphoreType.DMA
    anywhere = pl.BlockSpec(memory_space=pltpu.HBM)
    in_vmem = pl.BlockSpec(memory_space=pltpu.VMEM)
    parts = pl.pallas_call(
        functools.partial(band_kernel, tiles, slots // 2),
        out_shape=(
            jax.ShapeDtypeStruct((slots, half, points), f32),
            jax.ShapeDtypeStruct((2, 4, half, points), bf16),
            jax.ShapeDtypeStruct((3, half, points), f32),
        ),
        in_specs=[anywhere, anywhere, pl.BlockSpec(memory_space=pltpu.SMEM), anywhere, anywhere],
        out_specs=(in_vmem,) * 3,
        scratch_shapes=[
            pltpu.SMEM(band_mask.shape, jnp.int32),
            pltpu.SMEM(live_counts.shape, jnp.int32),
            dma((2,)),
            pltpu.VMEM((3, 2, depth_r, half), bf16),
            pltpu.VMEM((3, 2, depth_s, half), bf16),
            pltpu.VMEM((3, 4, half, depth_r), bf16),
            pltpu.VMEM((3, 4, half, depth_s), bf16),
            pltpu.VMEM((half, points), f32),
            pltpu.VMEM((half, points), f32),
            pltpu.VMEM((3, 8, half // 2, half), bf16),
            pltpu.VMEM((3, 8, half, half // 2), bf16),
            dma((2, 2)),
            dma((2, 4, 2)),
            dma((2, 4, 2)),
            dma((3, 2)),
            dma((2, 4)),
            dma,
            dma,
        ],
        compiler_params=pltpu.CompilerParams(
            collective_id=0, has_side_effects=True, vmem_limit_bytes=VMEM_MIB * 1024 * 1024),
    )(in_hbm(green_recv.reshape(depth_r, points)), in_hbm(green_shot.reshape(depth_s, points)), freq_bins,
      in_hbm(band_mask), in_hbm(live_counts))
    band = pl.pallas_call(
        functools.partial(store_kernel, tiles),
        out_shape=jax.ShapeDtypeStruct((slots, half, points), f32),
        in_specs=[in_vmem] * 3,
        out_specs=anywhere,
        scratch_shapes=[pltpu.VMEM((2, half, points), f32), dma((slots,))],
        compiler_params=pltpu.CompilerParams(vmem_limit_bytes=4 * 1024 * 1024),
    )(*parts)
    return jnp.transpose(band, (1, 0, 2))


def solution(mesh):
    return jax.shard_map(
        per_device,
        mesh=mesh,
        in_specs=(
            P(("grp", "freq"), None, None, "tile"),
            P(("grp", "freq"), None, None, "tile"),
            P("grp", None),
            P("grp"),
            P(("grp", "freq")),
        ),
        out_specs=P(("grp", "tile", "freq"), None, None),
        check_vma=False,
    )
```

```python
import functools

import jax
import jax.numpy as jnp
from jax import lax
from jax.experimental import pallas as pl
from jax.experimental.pallas import tpu as pltpu
from jax.sharding import PartitionSpec as P

BINS = 512
VMEM_MIB = 44
MESH = pl.DeviceIdType.MESH
PAIR = {(1, 0): 0, (2, 0): 1, (2, 1): 2, (1, 2): 2}
ROW = {1: 0, 2: 1, -1: 2, -2: 3}


def place(tiles):
    t = lax.axis_index("tile")
    f = lax.axis_index("freq")
    step = 1 - 2 * f
    r = f * (tiles - 1) + step * t
    return t, f, step, r, lax.rem(r, 2) == 0


def band_kernel(tiles, radius, recv_ref, shot_ref, bins_ref, band_hbm, live_hbm, out, inbox, own,
                band_ref, live_ref, table_sem, far_r, far_s, left_r, left_s, self_out, self_in, outbox, turned,
                own_sem, data_send, data_recv, res_send, res_recv, self_send, self_recv):
    t, f, step, r, heavy = place(tiles)
    depth_r, points = recv_ref.shape
    depth_s = shot_ref.shape[0]
    half = points // 2
    part = half // 2
    has_far = r + 2 < tiles
    tables = [pltpu.make_async_copy(src, dst, table_sem.at[k]) for k, (src, dst) in enumerate(
        ((band_hbm, band_ref), (live_hbm, live_ref)))]
    def columns(j):
        return pl.ds(pl.multiple_of(j * half, half), half)

    def parts(i):
        return pl.ds(pl.multiple_of(i * part, part), part)

    def own_copy(which, j):
        src, dst = ((recv_ref, far_r), (shot_ref, far_s))[which]
        return pltpu.make_async_copy(src.at[:, columns(j)], dst.at[0, j], own_sem.at[which, j])

    def data_copy(which, i, distance):
        src, dst = ((recv_ref, far_r), (shot_ref, far_s))[which]
        return pltpu.make_async_remote_copy(
            src_ref=src.at[:, parts(i)], dst_ref=dst.at[distance, i // 2, :, parts(i % 2)],
            send_sem=data_send.at[which, i, distance - 1], recv_sem=data_recv.at[which, i, distance - 1],
            device_id={"tile": t - step * distance}, device_id_type=MESH)

    barrier = pltpu.get_barrier_semaphore()

    def greet(tile, freq):
        pl.semaphore_signal(barrier, inc=1, device_id={"tile": tile, "freq": freq}, device_id_type=MESH)

    pl.when(has_far)(lambda: greet(t + 2 * step, f))
    pl.when(heavy)(lambda: greet(t + step, f))
    greet(t, 1 - f)
    greeters = 1 + jnp.where(heavy, 0, 1) + jnp.where(r >= 2, 1, 0)
    pl.semaphore_wait(barrier, greeters)

    for i in range(4):
        for which in range(2):
            @pl.when(jnp.logical_not(heavy))
            def _():
                data_copy(which, i, 1).start()

            @pl.when(r >= 2)
            def _():
                data_copy(which, i, 2).start()

    for table in tables:
        table.start()

    for j in range(2):
        for which in range(2):
            own_copy(which, j).start()

    def build_left(slot, i):
        for src, dst, depth in ((far_r, left_r, depth_r // 2), (far_s, left_s, depth_s // 2)):
            re = src[slot, i // 2, 0:depth, parts(i % 2)].T
            im = src[slot, i // 2, depth:2 * depth, parts(i % 2)].T
            dst[slot, i, 0:part, 0:depth] = re
            dst[slot, i, 0:part, depth:2 * depth] = im
            dst[slot, i, part:half, 0:depth] = im
            dst[slot, i, part:half, depth:2 * depth] = -re

    def block(left, i, right, h):
        rr = jnp.dot(left_r[left, i], far_r[right, h], preferred_element_type=jnp.float32)
        ss = jnp.dot(left_s[left, i], far_s[right, h], preferred_element_type=jnp.float32)
        return (rr[:part] * ss[:part] - rr[part:] * ss[part:]) * weight

    def origin_at(h):
        return jnp.where(h == f, 0, 1)

    def plain_send(left, i, right, h, n):
        k, origin, row = PAIR[left, right], origin_at(i // 2), ROW[right - left]
        return pltpu.make_async_remote_copy(
            src_ref=outbox.at[k, n], dst_ref=inbox.at[origin, row, parts(i % 2), columns(h)],
            send_sem=res_send.at[k, 0], recv_sem=res_recv.at[origin, row],
            device_id={"tile": t + step * left, "freq": i // 2}, device_id_type=MESH)

    def turned_send(left, i, right, h, n):
        k, origin, row = PAIR[left, right], origin_at(h), ROW[left - right]
        return pltpu.make_async_remote_copy(
            src_ref=turned.at[k, n], dst_ref=inbox.at[origin, row, :, parts(i)],
            send_sem=res_send.at[k, 1], recv_sem=res_recv.at[origin, row],
            device_id={"tile": t + step * right, "freq": h}, device_id_type=MESH)

    def unit(left, i, right, h, n, send):
        k = PAIR[left, right]
        value = block(left, i, right, h)
        outbox[k, n] = value.astype(jnp.bfloat16)
        if send:
            plain_send(left, i, right, h, n).start()
        if right == 0:
            @pl.when(h == f)
            def _():
                own[left, :, parts(i)] = value.T

            @pl.when(h != f)
            def _():
                turned[k, n] = value.T.astype(jnp.bfloat16)
                turned_send(left, i, right, h, n).start()
        else:
            turned[k, n] = value.T.astype(jnp.bfloat16)
            if send:
                turned_send(left, i, right, h, n).start()

    def self_copy():
        return pltpu.make_async_remote_copy(
            src_ref=self_out, dst_ref=self_in, send_sem=self_send, recv_sem=self_recv,
            device_id={"freq": 1 - f}, device_id_type=MESH)

    for j in range(2):
        for which in range(2):
            own_copy(which, j).wait()

    @pl.loop(0, 4)
    def _(i):
        build_left(0, i)

    for table in tables:
        table.wait()
    weight_root = bins_ref[0].astype(jnp.float32) / BINS
    weight = (weight_root * weight_root) * (weight_root * weight_root)

    for target, dest in ((1 - f, self_out), (f, own.at[0])):
        @pl.loop(0, 4)
        def _(m):
            dest[parts(m // 2), columns(m % 2)] = block(0, 2 * target + m // 2, 0, m % 2)

        if dest is self_out:
            self_copy().start()

    def mixed(first, bound, send):
        @pl.loop(first, bound)
        def _(n):
            unit(2, n // 2, 1, n % 2, n, send)

    @pl.loop(0, 3)
    def _(i):
        @pl.when(heavy)
        def _():
            for which in range(2):
                data_copy(which, i, 1).wait_recv()
            build_left(1, i)

            @pl.loop(0, 2)
            def _(h):
                unit(1, i, 0, h, 2 * i + h, False)

        @pl.when(heavy & has_far & (i == 2))
        def _():
            unit(1, i, 2, 0, 1, False)

        @pl.when(has_far)
        def _():
            for which in range(2):
                data_copy(which, i, 2).wait_recv()
            build_left(2, i)

            @pl.loop(0, 2)
            def _(h):
                unit(2, i, 0, h, 2 * i + h, False)

        @pl.when(heavy & has_far)
        def _():
            @pl.loop(0, jnp.where(i == 1, 2, jnp.where(i == 0, 0, 1)))
            def _(m):
                n = jnp.where(i == 1, 2 * m, 4)
                unit(2, n // 2, 1, n % 2, n, False)

    @pl.when(heavy)
    def _():
        data_copy(0, 3, 1).wait_recv()

        @pl.loop(0, 6)
        def _(n):
            plain_send(1, n // 2, 0, n % 2, n).start()

    @pl.when(has_far)
    def _():
        data_copy(0, 3, 2).wait_recv()

        def release():
            @pl.loop(0, 6)
            def _(n):
                plain_send(2, n // 2, 0, n % 2, n).start()

        pl.when(heavy)(release)

    @pl.when(heavy & has_far)
    def _():
        plain_send(1, 2, 2, 0, 1).start()
        turned_send(1, 2, 2, 0, 1).start()

        @pl.loop(0, 3)
        def _(m):
            plain_send(2, m, 1, 0, 2 * m).start()
            turned_send(2, m, 1, 0, 2 * m).start()

    @pl.when(heavy)
    def _():
        data_copy(1, 3, 1).wait_recv()
        build_left(1, 3)

        @pl.loop(0, 2)
        def _(h):
            unit(1, 3, 0, h, 6 + h, True)

    @pl.when(has_far)
    def _():
        data_copy(1, 3, 2).wait_recv()

        @pl.when(jnp.logical_not(heavy))
        def _():
            @pl.loop(0, 6)
            def _(n):
                plain_send(2, n // 2, 0, n % 2, n).start()

        @pl.when(heavy)
        def _():
            unit(1, 3, 2, 0, 3, True)

        build_left(2, 3)

        @pl.loop(0, 2)
        def _(h):
            unit(2, 3, 0, h, 6 + h, True)

        @pl.when(heavy)
        def _():
            @pl.loop(5, 8)
            def _(n):
                unit(2, n // 2, 1, n % 2, n, True)

    rows = lax.broadcasted_iota(jnp.int32, (half, points), 0) + f * half
    cols = lax.broadcasted_iota(jnp.int32, (half, points), 1)
    row_live = rows < live_ref[t]

    def wait_inbox(origin, row):
        pltpu.make_async_remote_copy(
            src_ref=inbox.at[origin, row], dst_ref=inbox.at[origin, row],
            send_sem=res_send.at[0, 0], recv_sem=res_recv.at[origin, row],
            device_id={"freq": 1 - f}, device_id_type=MESH).wait_recv()

    def kept(delta):
        near, slot = t + step * delta, radius + step * delta
        return slot, row_live & (cols < live_ref[near]) & (band_ref[t, slot] > 0)

    def emit(delta, value):
        slot, keep = kept(delta)
        out[slot] = jnp.where(keep, value, 0.0)

    for delta in (1, -1):
        @pl.when((r + delta >= 0) & (r + delta < tiles))
        def _():
            emit(delta, jnp.ones((half, points), jnp.float32))

    self_copy().wait_recv()
    emit(0, own[0] + self_in[...])
    for delta in (2, -2):
        row, mirror = ROW[delta], ROW[-delta]
        exists = (r + delta >= 0) & (r + delta < tiles)

        @pl.when(exists)
        def _():
            wait_inbox(1, mirror)
            if delta == 2:
                emit(delta, own[delta] + inbox[1, mirror].astype(jnp.float32))
            else:
                wait_inbox(0, row)
                emit(delta, inbox[0, row].astype(jnp.float32) + inbox[1, mirror].astype(jnp.float32))

        @pl.when(jnp.logical_not(exists))
        def _():
            out[radius + step * delta] = jnp.zeros((half, points), jnp.float32)

    for delta in (1, -1):
        @pl.when((r + delta >= 0) & (r + delta < tiles))
        def _():
            wait_inbox(1, ROW[-delta])
            if delta == 1:
                pl.when(jnp.logical_not(heavy))(lambda: wait_inbox(0, ROW[delta]))
            else:
                wait_inbox(0, ROW[delta])

    self_copy().wait_send()
    for i in range(4):
        for which in range(2):
            @pl.when(jnp.logical_not(heavy))
            def _():
                data_copy(which, i, 1).wait_send()

            @pl.when(r >= 2)
            def _():
                data_copy(which, i, 2).wait_send()

    def wait_sent(box, sem):
        pltpu.make_async_remote_copy(
            src_ref=box, dst_ref=box, send_sem=sem, recv_sem=res_recv.at[0, 0],
            device_id={"freq": 1 - f}, device_id_type=MESH).wait_send()

    for k, made in enumerate((heavy, has_far, heavy & has_far)):
        @pl.when(made)
        def _():
            wait_sent(outbox.at[k], res_send.at[k, 0])
            wait_sent(turned.at[k] if k == 2 else turned.at[k, 0:4], res_send.at[k, 1])


def store_kernel(tiles, band, inbox, own, out_ref, late, out_sem):
    t, f, step, r, heavy = place(tiles)
    slots, half, points = band.shape
    radius = slots // 2
    ready = [slot for slot in range(slots) if abs(slot - radius) != 1]
    copies = [pltpu.make_async_copy(band.at[slot], out_ref.at[slot], out_sem.at[slot]) for slot in ready]
    for copy in copies:
        copy.start()
    for k, delta in enumerate((1, -1)):
        slot = radius + step * delta
        exists = (r + delta >= 0) & (r + delta < tiles)

        def total(first):
            value = first + inbox[1, ROW[-delta]].astype(jnp.float32)
            late[k] = jnp.where(band[slot] > 0, value, 0.0)

        def from_inbox():
            total(inbox[0, ROW[delta]].astype(jnp.float32))

        if delta == 1:
            pl.when(exists & heavy)(lambda: total(own[1]))
            pl.when(exists & jnp.logical_not(heavy))(from_inbox)
        else:
            pl.when(exists)(from_inbox)

        @pl.when(jnp.logical_not(exists))
        def _():
            late[k] = jnp.zeros((half, points), jnp.float32)

        copies.append(pltpu.make_async_copy(late.at[k], out_ref.at[slot], out_sem.at[radius - 1 + 2 * k]))
        copies[-1].start()
    for copy in copies:
        copy.wait()


def in_hbm(array):
    return pltpu.with_memory_space_constraint(array, pltpu.HBM)


def per_device(green_recv, green_shot, band_mask, live_counts, freq_bins):
    tiles = lax.axis_size("tile")
    points = green_recv.shape[3]
    slots = band_mask.shape[1]
    half = points // 2
    depth_r = 2 * green_recv.shape[2]
    depth_s = 2 * green_shot.shape[2]
    bf16, f32 = jnp.bfloat16, jnp.float32
    dma = pltpu.SemaphoreType.DMA
    anywhere = pl.BlockSpec(memory_space=pltpu.HBM)
    in_vmem = pl.BlockSpec(memory_space=pltpu.VMEM)
    parts = pl.pallas_call(
        functools.partial(band_kernel, tiles, slots // 2),
        out_shape=(
            jax.ShapeDtypeStruct((slots, half, points), f32),
            jax.ShapeDtypeStruct((2, 4, half, points), bf16),
            jax.ShapeDtypeStruct((3, half, points), f32),
        ),
        in_specs=[anywhere, anywhere, pl.BlockSpec(memory_space=pltpu.SMEM), anywhere, anywhere],
        out_specs=(in_vmem,) * 3,
        scratch_shapes=[
            pltpu.SMEM(band_mask.shape, jnp.int32),
            pltpu.SMEM(live_counts.shape, jnp.int32),
            dma((2,)),
            pltpu.VMEM((3, 2, depth_r, half), bf16),
            pltpu.VMEM((3, 2, depth_s, half), bf16),
            pltpu.VMEM((3, 4, half, depth_r), bf16),
            pltpu.VMEM((3, 4, half, depth_s), bf16),
            pltpu.VMEM((half, points), f32),
            pltpu.VMEM((half, points), f32),
            pltpu.VMEM((3, 8, half // 2, half), bf16),
            pltpu.VMEM((3, 8, half, half // 2), bf16),
            dma((2, 2)),
            dma((2, 4, 2)),
            dma((2, 4, 2)),
            dma((3, 2)),
            dma((2, 4)),
            dma,
            dma,
        ],
        compiler_params=pltpu.CompilerParams(
            collective_id=0, has_side_effects=True, vmem_limit_bytes=VMEM_MIB * 1024 * 1024),
    )(in_hbm(green_recv.reshape(depth_r, points)), in_hbm(green_shot.reshape(depth_s, points)), freq_bins,
      in_hbm(band_mask), in_hbm(live_counts))
    band = pl.pallas_call(
        functools.partial(store_kernel, tiles),
        out_shape=jax.ShapeDtypeStruct((slots, half, points), f32),
        in_specs=[in_vmem] * 3,
        out_specs=anywhere,
        scratch_shapes=[pltpu.VMEM((2, half, points), f32), dma((slots,))],
        compiler_params=pltpu.CompilerParams(vmem_limit_bytes=4 * 1024 * 1024),
    )(*parts)
    return jnp.transpose(band, (1, 0, 2))


def solution(mesh):
    return jax.shard_map(
        per_device,
        mesh=mesh,
        in_specs=(
            P(("grp", "freq"), None, None, "tile"),
            P(("grp", "freq"), None, None, "tile"),
            P("grp", None),
            P("grp"),
            P(("grp", "freq")),
        ),
        out_specs=P(("grp", "tile", "freq"), None, None),
        check_vma=False,
    )
```

```python
import functools

import jax
import jax.numpy as jnp
from jax import lax
from jax.experimental import pallas as pl
from jax.experimental.pallas import tpu as pltpu
from jax.sharding import PartitionSpec as P

BINS = 512
VMEM_MIB = 44
MESH = pl.DeviceIdType.MESH
PAIR = {(1, 0): 0, (2, 0): 1, (2, 1): 2, (1, 2): 2}
ROW = {1: 0, 2: 1, -1: 2, -2: 3}


def place(tiles):
    t = lax.axis_index("tile")
    f = lax.axis_index("freq")
    step = 1 - 2 * f
    r = f * (tiles - 1) + step * t
    return t, f, step, r, lax.rem(r, 2) == 0


def band_kernel(tiles, radius, recv_ref, shot_ref, bins_ref, band_hbm, live_hbm, out, inbox, own,
                band_ref, live_ref, table_sem, far_r, far_s, left_r, left_s, self_out, self_in, outbox, turned,
                own_sem, data_send, data_recv, res_send, res_recv, self_send, self_recv):
    t, f, step, r, heavy = place(tiles)
    depth_r, points = recv_ref.shape
    depth_s = shot_ref.shape[0]
    half = points // 2
    part = half // 2
    has_far = r + 2 < tiles
    tables = [pltpu.make_async_copy(src, dst, table_sem.at[k]) for k, (src, dst) in enumerate(
        ((band_hbm, band_ref), (live_hbm, live_ref)))]
    for table in tables:
        table.start()

    def columns(j):
        return pl.ds(pl.multiple_of(j * half, half), half)

    def parts(i):
        return pl.ds(pl.multiple_of(i * part, part), part)

    def own_copy(which, j):
        src, dst = ((recv_ref, far_r), (shot_ref, far_s))[which]
        return pltpu.make_async_copy(src.at[:, columns(j)], dst.at[0, j], own_sem.at[which, j])

    def data_copy(which, i, distance):
        src, dst = ((recv_ref, far_r), (shot_ref, far_s))[which]
        return pltpu.make_async_remote_copy(
            src_ref=src.at[:, parts(i)], dst_ref=dst.at[distance, i // 2, :, parts(i % 2)],
            send_sem=data_send.at[which, i, distance - 1], recv_sem=data_recv.at[which, i, distance - 1],
            device_id={"tile": t - step * distance}, device_id_type=MESH)

    barrier = pltpu.get_barrier_semaphore()

    def greet(tile, freq):
        pl.semaphore_signal(barrier, inc=1, device_id={"tile": tile, "freq": freq}, device_id_type=MESH)

    pl.when(has_far)(lambda: greet(t + 2 * step, f))
    pl.when(heavy)(lambda: greet(t + step, f))
    greet(t, 1 - f)
    greeters = 1 + jnp.where(heavy, 0, 1) + jnp.where(r >= 2, 1, 0)
    for j in range(2):
        for which in range(2):
            own_copy(which, j).start()

    pl.semaphore_wait(barrier, greeters)

    for i in range(4):
        for which in range(2):
            @pl.when(jnp.logical_not(heavy))
            def _():
                data_copy(which, i, 1).start()

            @pl.when(r >= 2)
            def _():
                data_copy(which, i, 2).start()

    def build_left(slot, i):
        for src, dst, depth in ((far_r, left_r, depth_r // 2), (far_s, left_s, depth_s // 2)):
            re = src[slot, i // 2, 0:depth, parts(i % 2)].T
            im = src[slot, i // 2, depth:2 * depth, parts(i % 2)].T
            dst[slot, i, 0:part, 0:depth] = re
            dst[slot, i, 0:part, depth:2 * depth] = im
            dst[slot, i, part:half, 0:depth] = im
            dst[slot, i, part:half, depth:2 * depth] = -re

    def block(left, i, right, h):
        rr = jnp.dot(left_r[left, i], far_r[right, h], preferred_element_type=jnp.float32)
        ss = jnp.dot(left_s[left, i], far_s[right, h], preferred_element_type=jnp.float32)
        return (rr[:part] * ss[:part] - rr[part:] * ss[part:]) * weight

    def origin_at(h):
        return jnp.where(h == f, 0, 1)

    def plain_send(left, i, right, h, n):
        k, origin, row = PAIR[left, right], origin_at(i // 2), ROW[right - left]
        return pltpu.make_async_remote_copy(
            src_ref=outbox.at[k, n], dst_ref=inbox.at[origin, row, parts(i % 2), columns(h)],
            send_sem=res_send.at[k, 0], recv_sem=res_recv.at[origin, row],
            device_id={"tile": t + step * left, "freq": i // 2}, device_id_type=MESH)

    def turned_send(left, i, right, h, n):
        k, origin, row = PAIR[left, right], origin_at(h), ROW[left - right]
        return pltpu.make_async_remote_copy(
            src_ref=turned.at[k, n], dst_ref=inbox.at[origin, row, :, parts(i)],
            send_sem=res_send.at[k, 1], recv_sem=res_recv.at[origin, row],
            device_id={"tile": t + step * right, "freq": h}, device_id_type=MESH)

    def unit(left, i, right, h, n, send):
        k = PAIR[left, right]
        value = block(left, i, right, h)
        outbox[k, n] = value.astype(jnp.bfloat16)
        if send:
            plain_send(left, i, right, h, n).start()
        if right == 0:
            @pl.when(h == f)
            def _():
                own[left, :, parts(i)] = value.T

            @pl.when(h != f)
            def _():
                turned[k, n] = value.T.astype(jnp.bfloat16)
                turned_send(left, i, right, h, n).start()
        else:
            turned[k, n] = value.T.astype(jnp.bfloat16)
            if send:
                turned_send(left, i, right, h, n).start()

    def self_copy():
        return pltpu.make_async_remote_copy(
            src_ref=self_out, dst_ref=self_in, send_sem=self_send, recv_sem=self_recv,
            device_id={"freq": 1 - f}, device_id_type=MESH)

    for j in range(2):
        for which in range(2):
            own_copy(which, j).wait()

    @pl.loop(0, 4)
    def _(i):
        build_left(0, i)

    for table in tables:
        table.wait()
    weight_root = bins_ref[0].astype(jnp.float32) / BINS
    weight = (weight_root * weight_root) * (weight_root * weight_root)

    for target, dest in ((1 - f, self_out), (f, own.at[0])):
        @pl.loop(0, 4)
        def _(m):
            dest[parts(m // 2), columns(m % 2)] = block(0, 2 * target + m // 2, 0, m % 2)

        if dest is self_out:
            self_copy().start()

    def mixed(first, bound, send):
        @pl.loop(first, bound)
        def _(n):
            unit(2, n // 2, 1, n % 2, n, send)

    @pl.loop(0, 3)
    def _(i):
        @pl.when(heavy)
        def _():
            for which in range(2):
                data_copy(which, i, 1).wait_recv()
            build_left(1, i)

            @pl.loop(0, 2)
            def _(h):
                unit(1, i, 0, h, 2 * i + h, False)

        @pl.when(heavy & has_far & (i == 2))
        def _():
            unit(1, i, 2, 0, 1, False)

        @pl.when(has_far)
        def _():
            for which in range(2):
                data_copy(which, i, 2).wait_recv()
            build_left(2, i)

            @pl.loop(0, 2)
            def _(h):
                unit(2, i, 0, h, 2 * i + h, False)

        @pl.when(heavy & has_far)
        def _():
            @pl.loop(0, jnp.where(i == 1, 2, jnp.where(i == 0, 0, 1)))
            def _(m):
                n = jnp.where(i == 1, 2 * m, 4)
                unit(2, n // 2, 1, n % 2, n, False)

    @pl.when(heavy)
    def _():
        data_copy(0, 3, 1).wait_recv()

        @pl.loop(0, 6)
        def _(n):
            plain_send(1, n // 2, 0, n % 2, n).start()

    @pl.when(has_far)
    def _():
        data_copy(0, 3, 2).wait_recv()

        @pl.loop(0, 6)
        def _(n):
            plain_send(2, n // 2, 0, n % 2, n).start()

    @pl.when(heavy & has_far)
    def _():
        plain_send(1, 2, 2, 0, 1).start()
        turned_send(1, 2, 2, 0, 1).start()

        @pl.loop(0, 3)
        def _(m):
            plain_send(2, m, 1, 0, 2 * m).start()
            turned_send(2, m, 1, 0, 2 * m).start()

    @pl.when(heavy)
    def _():
        data_copy(1, 3, 1).wait_recv()
        build_left(1, 3)

        @pl.loop(0, 2)
        def _(h):
            unit(1, 3, 0, h, 6 + h, True)

    @pl.when(has_far)
    def _():
        data_copy(1, 3, 2).wait_recv()

        @pl.when(heavy)
        def _():
            unit(1, 3, 2, 0, 3, True)

        build_left(2, 3)

        @pl.loop(0, 2)
        def _(h):
            unit(2, 3, 0, h, 6 + h, True)

        @pl.when(heavy)
        def _():
            @pl.loop(5, 8)
            def _(n):
                unit(2, n // 2, 1, n % 2, n, True)

    rows = lax.broadcasted_iota(jnp.int32, (half, points), 0) + f * half
    cols = lax.broadcasted_iota(jnp.int32, (half, points), 1)
    row_live = rows < live_ref[t]

    def wait_inbox(origin, row):
        pltpu.make_async_remote_copy(
            src_ref=inbox.at[origin, row], dst_ref=inbox.at[origin, row],
            send_sem=res_send.at[0, 0], recv_sem=res_recv.at[origin, row],
            device_id={"freq": 1 - f}, device_id_type=MESH).wait_recv()

    def kept(delta):
        near, slot = t + step * delta, radius + step * delta
        return slot, row_live & (cols < live_ref[near]) & (band_ref[t, slot] > 0)

    def emit(delta, value):
        slot, keep = kept(delta)
        out[slot] = jnp.where(keep, value, 0.0)

    for delta in (1, -1):
        @pl.when((r + delta >= 0) & (r + delta < tiles))
        def _():
            emit(delta, jnp.ones((half, points), jnp.float32))

    self_copy().wait_recv()
    emit(0, own[0] + self_in[...])
    self_copy().wait_send()
    for i in range(4):
        for which in range(2):
            @pl.when(jnp.logical_not(heavy))
            def _():
                data_copy(which, i, 1).wait_send()

            @pl.when(r >= 2)
            def _():
                data_copy(which, i, 2).wait_send()

    for delta in (2, -2):
        row, mirror = ROW[delta], ROW[-delta]
        exists = (r + delta >= 0) & (r + delta < tiles)

        @pl.when(exists)
        def _():
            wait_inbox(1, mirror)
            if delta == 2:
                emit(delta, own[delta] + inbox[1, mirror].astype(jnp.float32))
            else:
                wait_inbox(0, row)
                emit(delta, inbox[0, row].astype(jnp.float32) + inbox[1, mirror].astype(jnp.float32))

        @pl.when(jnp.logical_not(exists))
        def _():
            out[radius + step * delta] = jnp.zeros((half, points), jnp.float32)

    for delta in (1, -1):
        @pl.when((r + delta >= 0) & (r + delta < tiles))
        def _():
            wait_inbox(1, ROW[-delta])
            if delta == 1:
                pl.when(jnp.logical_not(heavy))(lambda: wait_inbox(0, ROW[delta]))
            else:
                wait_inbox(0, ROW[delta])

    def wait_sent(box, sem):
        pltpu.make_async_remote_copy(
            src_ref=box, dst_ref=box, send_sem=sem, recv_sem=res_recv.at[0, 0],
            device_id={"freq": 1 - f}, device_id_type=MESH).wait_send()

    for k, made in enumerate((heavy, has_far, heavy & has_far)):
        @pl.when(made)
        def _():
            wait_sent(outbox.at[k], res_send.at[k, 0])
            wait_sent(turned.at[k] if k == 2 else turned.at[k, 0:4], res_send.at[k, 1])


def store_kernel(tiles, band, inbox, own, out_ref, late, out_sem):
    t, f, step, r, heavy = place(tiles)
    slots, half, points = band.shape
    radius = slots // 2
    ready = [slot for slot in range(slots) if abs(slot - radius) != 1]
    copies = [pltpu.make_async_copy(band.at[slot], out_ref.at[slot], out_sem.at[slot]) for slot in ready]
    for copy in copies:
        copy.start()
    for k, delta in enumerate((1, -1)):
        slot = radius + step * delta
        exists = (r + delta >= 0) & (r + delta < tiles)

        def total(first):
            value = first + inbox[1, ROW[-delta]].astype(jnp.float32)
            late[k] = jnp.where(band[slot] > 0, value, 0.0)

        def from_inbox():
            total(inbox[0, ROW[delta]].astype(jnp.float32))

        if delta == 1:
            pl.when(exists & heavy)(lambda: total(own[1]))
            pl.when(exists & jnp.logical_not(heavy))(from_inbox)
        else:
            pl.when(exists)(from_inbox)

        @pl.when(jnp.logical_not(exists))
        def _():
            late[k] = jnp.zeros((half, points), jnp.float32)

        copies.append(pltpu.make_async_copy(late.at[k], out_ref.at[slot], out_sem.at[radius - 1 + 2 * k]))
        copies[-1].start()
    for copy in copies:
        copy.wait()


def in_hbm(array):
    return pltpu.with_memory_space_constraint(array, pltpu.HBM)


def per_device(green_recv, green_shot, band_mask, live_counts, freq_bins):
    tiles = lax.axis_size("tile")
    points = green_recv.shape[3]
    slots = band_mask.shape[1]
    half = points // 2
    depth_r = 2 * green_recv.shape[2]
    depth_s = 2 * green_shot.shape[2]
    bf16, f32 = jnp.bfloat16, jnp.float32
    dma = pltpu.SemaphoreType.DMA
    anywhere = pl.BlockSpec(memory_space=pltpu.HBM)
    in_vmem = pl.BlockSpec(memory_space=pltpu.VMEM)
    parts = pl.pallas_call(
        functools.partial(band_kernel, tiles, slots // 2),
        out_shape=(
            jax.ShapeDtypeStruct((slots, half, points), f32),
            jax.ShapeDtypeStruct((2, 4, half, points), bf16),
            jax.ShapeDtypeStruct((3, half, points), f32),
        ),
        in_specs=[anywhere, anywhere, pl.BlockSpec(memory_space=pltpu.SMEM), anywhere, anywhere],
        out_specs=(in_vmem,) * 3,
        scratch_shapes=[
            pltpu.SMEM(band_mask.shape, jnp.int32),
            pltpu.SMEM(live_counts.shape, jnp.int32),
            dma((2,)),
            pltpu.VMEM((3, 2, depth_r, half), bf16),
            pltpu.VMEM((3, 2, depth_s, half), bf16),
            pltpu.VMEM((3, 4, half, depth_r), bf16),
            pltpu.VMEM((3, 4, half, depth_s), bf16),
            pltpu.VMEM((half, points), f32),
            pltpu.VMEM((half, points), f32),
            pltpu.VMEM((3, 8, half // 2, half), bf16),
            pltpu.VMEM((3, 8, half, half // 2), bf16),
            dma((2, 2)),
            dma((2, 4, 2)),
            dma((2, 4, 2)),
            dma((3, 2)),
            dma((2, 4)),
            dma,
            dma,
        ],
        compiler_params=pltpu.CompilerParams(
            collective_id=0, has_side_effects=True, vmem_limit_bytes=VMEM_MIB * 1024 * 1024),
    )(in_hbm(green_recv.reshape(depth_r, points)), in_hbm(green_shot.reshape(depth_s, points)), freq_bins,
      in_hbm(band_mask), in_hbm(live_counts))
    band = pl.pallas_call(
        functools.partial(store_kernel, tiles),
        out_shape=jax.ShapeDtypeStruct((slots, half, points), f32),
        in_specs=[in_vmem] * 3,
        out_specs=anywhere,
        scratch_shapes=[pltpu.VMEM((2, half, points), f32), dma((slots,))],
        compiler_params=pltpu.CompilerParams(vmem_limit_bytes=4 * 1024 * 1024),
    )(*parts)
    return jnp.transpose(band, (1, 0, 2))


def solution(mesh):
    return jax.shard_map(
        per_device,
        mesh=mesh,
        in_specs=(
            P(("grp", "freq"), None, None, "tile"),
            P(("grp", "freq"), None, None, "tile"),
            P("grp", None),
            P("grp"),
            P(("grp", "freq")),
        ),
        out_specs=P(("grp", "tile", "freq"), None, None),
        check_vma=False,
    )
```
